32 devices in a mesh: paths: 4 (over y, core), factors: 8 (over z, x).
Axes of the slice: x: 2, y: 2, z: 4, core: 2. Of those that a mesh axis runs over, the one named last changes fastest.
Arguments:
- x_start: float32 [512, 2048], P('factors', 'paths'), may hold values from -3 to 3
- shocks: float32 [4, 512, 2048], P(None, 'factors', 'paths'), may hold values from -6 to 6
- cholesky: float32 [512, 512], P(None, 'factors'), as said below
- reversion: float32 [512], P('factors'), may hold values from 0.05 to 2
- sabr_alpha: float32 [64], replicated, may hold values from 0.2 to 0.6
- sabr_rho: float32 [64], replicated, may hold values from -0.7 to 0.7
- sabr_nu: float32 [64], replicated, may hold values from 0.3 to 1.5
- factor_slice: int32 [512], P('factors'), may hold values from 0 to 63
- notional: float32 [32768], P('factors'), may hold values from -1 to 1
- strike: float32 [32768], P('factors'), may hold values from -3 to 3
- trade_set: int32 [32768], P('factors'), may hold values from 0 to 255
- trade_factor: int32 [32768], P('factors'), may hold values from 0 to 511, as said below
- loss_given: float32 [256], replicated, may hold values from 0.2 to 0.8
Outputs:
- path_adjoint: float32 [512, 2048], P('factors', 'paths')
- sabr_grad: float32 [3, 64], replicated
The draws below stay inside these ranges and needn't reach their ends.
Inputs may be any that keep to these rules, and one draw needn't show every extreme that they name: `cholesky`: lower triangular with a positive diagonal and rows of unit length. `trade_factor`: trade t's factor lies in [(t // 4096) * 64, (t // 4096 + 1) * 64).
All inputs are finite; a program needn't handle non-finite values.
Results may differ from the reference program's by a relative error of at most 0.004.
Values may be sent and summed in bfloat16 or wider, within the bound.
A program may use at most 192 MiB of HBM per device.

```python
import math
import jax
import jax.numpy as jnp
import numpy as np
from jax import lax

F = 512
SLICES = 64
STEPS = 4
P_DEV = 512
TRADES_DEV = 4096
F_DEV = 64
NPATHS = 2048
TRADES = 32768
NSETS = 256
N_PATHS = 4


def draw_cholesky(key, part):
    subkeys = jax.random.split(jax.random.fold_in(key, 11), 4)
    normal_draw = jax.random.normal(subkeys[0], (F, F), jnp.float32)
    row_index = jnp.arange(F)[:, None]
    col_index = jnp.arange(F)[None, :]
    strict_lower = jnp.where(col_index < row_index, normal_draw / jnp.sqrt(jnp.maximum(row_index, 1).astype(jnp.float32)), 0.0)
    row_loading = jax.random.uniform(subkeys[2], (F, 1), jnp.float32, 0.5, 1.5)
    col_sign = jnp.where(jax.random.uniform(subkeys[3], (1, F), jnp.float32) < 0.5, -1.0, 1.0)
    sector = jnp.where((col_index < row_index) & (col_index < F_DEV), 0.8 * row_loading * col_sign / jnp.sqrt(jnp.float32(F_DEV)), 0.0)
    diagonal = jax.random.uniform(subkeys[1], (F,), jnp.float32, 0.5, 1.5)
    triangle = strict_lower + sector + jnp.diag(diagonal)
    return triangle / jnp.sqrt(jnp.sum(triangle * triangle, axis=1, keepdims=True))


def draw_trade_factor(key, part):
    position = jnp.arange(TRADES, dtype=jnp.int32)
    within = position % TRADES_DEV
    offset = jax.random.randint(jax.random.fold_in(key, 23), (TRADES,), 0, F_DEV, dtype=jnp.int32)
    offset = jnp.where(within == 0, 0, jnp.where(within == TRADES_DEV - 1, F_DEV - 1, offset))
    return (position // TRADES_DEV * F_DEV + offset).astype(jnp.int32)


def touch_ends(result, own_key, low, top_value):
    spot = [jax.random.randint(jax.random.fold_in(own_key, axis), (), 0, length) for axis, length in enumerate(result.shape)]
    widest = result.shape.index(max(result.shape))
    beside = spot[:widest] + [(spot[widest] + 1) % result.shape[widest]] + spot[widest + 1:]
    return result.at[tuple(spot)].set(low).at[tuple(beside)].set(top_value)


def steps_of(own_key, shape, shards, smallest, high):
    loudness, own = 1.0, jax.random.fold_in(own_key, 6)
    for axis_at, blocks in shards:
        steps = jnp.exp(jax.random.uniform(jax.random.fold_in(own, axis_at), (blocks,), jnp.float32, smallest / len(shards), high / len(shards)))
        loudness = loudness * jnp.repeat(steps, shape[axis_at] // blocks).reshape([-1 if axis == axis_at else 1 for axis in range(len(shape))])
    return loudness


def rank_bounds(amount, slope):
    loads = [(1 << 20) // math.isqrt(grade ** slope) + 1 for grade in range(1, amount + 1)]
    width = 1 + sum(loads) // (1 << 30)
    return np.cumsum(np.array([max(1, weight // width) for weight in loads]))


def ranked_ids(key, extent, number_of, slope):
    listing = rank_bounds(number_of, slope)
    pick = jax.random.randint(jax.random.fold_in(key, 1), extent, 0, int(listing[number_of - 1]))
    standing = jnp.searchsorted(jnp.asarray(listing, jnp.int32), pick, side="right")
    return jax.random.permutation(jax.random.fold_in(key, 2), number_of)[standing].astype(jnp.int32)


def centred(stream_key, dims, scale, limit, shards=(), kind=jnp.bfloat16):
    result = jax.random.normal(stream_key, dims, jnp.float32) * scale
    if len(shards) > 0:
        result = steps_of(stream_key, dims, shards, -0.22, 0.18) * result
    return jnp.clip(result, min=-limit, max=limit).astype(kind)


def setup_inputs(seed: int = 0) -> dict:
    key_list = jax.random.split(jax.random.key(seed), 14)
    return {
        "x_start": centred(key_list[0], (F, NPATHS), 0.5, 3.0, ((0, 8), (1, 4)), jnp.float32),
        "shocks": centred(key_list[1], (STEPS, F, NPATHS), 1.0, 6.0, ((1, 8), (2, 4)), jnp.float32),
        "cholesky": draw_cholesky(jax.random.fold_in(key_list[13], 71), 0),
        "reversion": jnp.clip(jnp.exp(math.log(2.0) - 3.6888794 * jax.random.uniform(key_list[3], (F,), jnp.float32) ** steps_of(key_list[3], (F,), ((0, 8),), -0.2, 0.2)), 0.05, 2.0),
        "sabr_alpha": jnp.clip(jax.random.uniform(key_list[4], (SLICES,), jnp.float32, 0.2, 0.6), 0.2, 0.6),
        "sabr_rho": jnp.clip(jax.random.uniform(key_list[5], (SLICES,), jnp.float32, -0.7, 0.7), -0.7, 0.7),
        "sabr_nu": jnp.clip(jnp.exp(jax.random.uniform(key_list[6], (SLICES,), jnp.float32, math.log(0.3), math.log(1.5))), 0.3, 1.5),
        "factor_slice": touch_ends(jax.random.randint(key_list[7], (F,), 0, SLICES), jax.random.fold_in(key_list[7], 1), 0, SLICES - 1).astype(jnp.int32),
        "notional": centred(key_list[8], (TRADES,), 0.15, 1.0, ((0, 8),), jnp.float32),
        "strike": centred(key_list[9], (TRADES,), 0.5, 3.0, ((0, 8),), jnp.float32),
        "trade_set": touch_ends(ranked_ids(key_list[10], (TRADES,), NSETS, 2), jax.random.fold_in(key_list[10], 3), 0, NSETS - 1).astype(jnp.int32),
        "trade_factor": draw_trade_factor(jax.random.fold_in(key_list[13], 71), 0),
        "loss_given": jnp.clip(jax.random.uniform(key_list[12], (NSETS,), jnp.float32, 0.2, 0.8), 0.2, 0.8),
    }


TIME_STEP = 0.25
ROOT_STEP = 0.5
DISCOUNT_RATE = 0.03
PRECISE = lax.Precision.HIGHEST


def smile_terms(squashed, alpha_rows, rho_rows, nu_rows):
    curve = (2.0 - 3.0 * rho_rows * rho_rows) * nu_rows * nu_rows / 24.0
    base = 1.0 + 0.5 * rho_rows * nu_rows * squashed + curve * squashed * squashed
    rho_slope = alpha_rows * (0.5 * nu_rows * squashed - 0.25 * rho_rows * nu_rows * nu_rows * squashed * squashed)
    nu_slope = alpha_rows * (0.5 * rho_rows * squashed + (2.0 - 3.0 * rho_rows * rho_rows) * nu_rows * squashed * squashed / 12.0)
    level_slope = alpha_rows * (0.5 * rho_rows * nu_rows + 2.0 * curve * squashed)
    return alpha_rows * base, base, rho_slope, nu_slope, level_slope


def reference(x_start, shocks, cholesky, reversion, sabr_alpha, sabr_rho, sabr_nu, factor_slice, notional, strike, trade_set, trade_factor, loss_given):
    alpha_rows = sabr_alpha[factor_slice][:, None]
    rho_rows = sabr_rho[factor_slice][:, None]
    nu_rows = sabr_nu[factor_slice][:, None]
    damping = (1.0 - reversion * TIME_STEP)[:, None]
    blocks = N_PATHS
    block_width = P_DEV
    starts = x_start.reshape(F, blocks, block_width).transpose(1, 0, 2)
    shock_blocks = shocks.reshape(STEPS, F, blocks, block_width).transpose(2, 0, 1, 3)

    def run_block(block_pair):
        state, shock_block = block_pair
        states = [state]
        weights = []
        for step_index in range(STEPS):
            squashed = jnp.tanh(state)
            local_vol = smile_terms(squashed, alpha_rows, rho_rows, nu_rows)[0]
            mixed = jnp.dot(cholesky, local_vol * shock_block[step_index], precision=PRECISE)
            state = damping * state + ROOT_STEP * mixed
            states.append(state)
            moneyness = jnp.take(state, trade_factor, axis=0) - strike[:, None]
            values = (notional[:, None] * jnp.tanh(moneyness)).astype(jnp.bfloat16)
            exposure = jax.ops.segment_sum(values.astype(jnp.float32), trade_set, num_segments=NSETS)
            discount = math.exp(-DISCOUNT_RATE * TIME_STEP * (step_index + 1))
            weights.append((discount * loss_given[:, None] * jax.nn.sigmoid(exposure)).astype(jnp.bfloat16))
        adjoint = jnp.zeros_like(state)
        factor_sums = jnp.zeros((3, F), jnp.float32)
        for step_index in reversed(range(STEPS)):
            moneyness = jnp.take(states[step_index + 1], trade_factor, axis=0) - strike[:, None]
            squash_trade = jnp.tanh(moneyness)
            trade_adjoint = jnp.take(weights[step_index].astype(jnp.float32), trade_set, axis=0)
            trade_term = notional[:, None] * (1.0 - squash_trade * squash_trade) * trade_adjoint
            adjoint = adjoint + jax.ops.segment_sum(trade_term, trade_factor, num_segments=F)
            shock_adjoint = jnp.dot(cholesky.T, ROOT_STEP * adjoint, precision=PRECISE)
            squashed = jnp.tanh(states[step_index])
            local_vol, base, rho_slope, nu_slope, level_slope = smile_terms(squashed, alpha_rows, rho_rows, nu_rows)
            vol_adjoint = shock_adjoint * shock_block[step_index]
            factor_sums = factor_sums + jnp.stack([jnp.sum(vol_adjoint * base, axis=1), jnp.sum(vol_adjoint * rho_slope, axis=1), jnp.sum(vol_adjoint * nu_slope, axis=1)])
            adjoint = damping * adjoint + vol_adjoint * level_slope * (1.0 - squashed * squashed)
        return adjoint, factor_sums

    adjoints, sums = lax.map(run_block, (starts, shock_blocks))
    path_adjoint = adjoints.transpose(1, 0, 2).reshape(F, blocks * block_width)
    factor_sums = jnp.sum(sums, axis=0)
    sabr_grad = jax.ops.segment_sum(factor_sums.T, factor_slice, num_segments=SLICES).T / (blocks * block_width)
    return path_adjoint, sabr_grad
```

```python
import functools
import math

import jax
import jax.numpy as jnp
from jax import lax
from jax.experimental import pallas as pl
from jax.experimental.pallas import tpu as pltpu
from jax.sharding import PartitionSpec as P

TIME_STEP = 0.25
ROOT_STEP = 0.5
DISCOUNT_RATE = 0.03
PRECISE = lax.Precision.HIGHEST
NN = (((1,), (0,)), ((), ()))
NT = (((1,), (1,)), ((), ()))
TILE = 512


def mm(a, b, dims):
    return lax.dot_general(a, b, dims, preferred_element_type=jnp.float32)


def split_mm(a, b, dims):
    rows = a.shape[0]
    high = a.astype(jnp.bfloat16)
    low = (a - high.astype(jnp.float32)).astype(jnp.bfloat16)
    both = mm(jnp.concatenate([high, low], axis=0), b, dims)
    return both[:rows] + both[rows:]


def one_hot(ids, count):
    rows = lax.broadcasted_iota(jnp.int32, (count, ids.shape[1]), 0).astype(jnp.float32)
    return jnp.where(rows == ids, 1.0, 0.0).astype(jnp.bfloat16)


def local_kernel(
    xs_ref,
    lt_ref,
    par_ref,
    trades_ref,
    loss_ref,
    a_ref,
    g_ref,
    states,
    parts,
    slopes,
    exposure,
    terms,
):
    steps = xs_ref.shape[0] - 1
    paths = xs_ref.shape[1]
    blocks, rows, part_width = parts.shape
    width = part_width // 3
    tiles = trades_ref.shape[0]
    per_block = tiles // blocks
    sets = loss_ref.shape[1]
    slices = g_ref.shape[1]

    alpha, rho, nu = par_ref[0:1, :], par_ref[1:2, :], par_ref[2:3, :]
    damping = 1.0 - par_ref[3:4, :] * TIME_STEP
    curve2 = 2.0 - 3.0 * rho * rho
    curve = curve2 * nu * nu / 24.0
    tilt = 0.5 * rho * nu

    state = xs_ref[0]
    for k in range(steps):
        states[k] = state
        u = jnp.tanh(state)
        source = alpha * (1.0 + tilt * u + curve * u * u) * xs_ref[k + 1]
        state = damping * state + ROOT_STEP * split_mm(source, lt_ref[...], NN)
        high = state.astype(jnp.bfloat16)
        rest = state - high.astype(jnp.float32)
        mid = rest.astype(jnp.bfloat16)
        low = (rest - mid.astype(jnp.float32)).astype(jnp.bfloat16)
        for b in range(blocks):
            cols = slice(b * width, (b + 1) * width)
            parts[b, k * paths : (k + 1) * paths, :] = jnp.concatenate(
                [high[:, cols], mid[:, cols], low[:, cols]], axis=1
            )

    exposure[...] = jnp.zeros_like(exposure)

    def forward(i, carry):
        b = i // per_block
        notional = trades_ref[i, 0:1, :]
        strike = trades_ref[i, 1:2, :]
        table = one_hot(trades_ref[i, 3:4, :], width)
        money = mm(parts[b], jnp.concatenate([table, table, table], axis=0), NN) - strike
        squash = jnp.tanh(money)
        value = notional * squash
        slopes[i] = (notional - value * squash).astype(jnp.bfloat16)
        set_table = one_hot(trades_ref[i, 2:3, :], sets)
        exposure[...] += mm(value.astype(jnp.bfloat16), set_table, NT)
        return carry

    lax.fori_loop(0, tiles, forward, 0)

    weights = jnp.concatenate(
        [
            math.exp(-DISCOUNT_RATE * TIME_STEP * (k + 1))
            * loss_ref[...]
            * jax.nn.sigmoid(exposure[k * paths : (k + 1) * paths, :])
            for k in range(steps)
        ],
        axis=0,
    ).astype(jnp.bfloat16)
    terms[...] = jnp.zeros_like(terms)

    def backward(i, carry):
        b = i // per_block
        set_table = one_hot(trades_ref[i, 2:3, :], sets)
        pulled = slopes[i].astype(jnp.float32) * mm(weights, set_table, NN)
        table = one_hot(trades_ref[i, 3:4, :], width)
        terms[b] += mm(pulled.astype(jnp.bfloat16), table, NT)
        return carry

    lax.fori_loop(0, tiles, backward, 0)

    adjoint = jnp.zeros_like(state)
    sums = [jnp.zeros((1, state.shape[1]), jnp.float32) for _ in range(3)]
    for k in reversed(range(steps)):
        adjoint = adjoint + jnp.concatenate(
            [terms[b, k * paths : (k + 1) * paths, :] for b in range(blocks)], axis=1
        )
        u = jnp.tanh(states[k])
        vbar = split_mm(ROOT_STEP * adjoint, lt_ref[...], NT) * xs_ref[k + 1]
        for at, slope in enumerate(
            (
                1.0 + tilt * u + curve * u * u,
                alpha * (0.5 * nu * u - 0.25 * rho * nu * nu * u * u),
                alpha * (0.5 * rho * u + curve2 * nu * u * u / 12.0),
            )
        ):
            sums[at] = sums[at] + jnp.sum(vbar * slope, axis=0, keepdims=True)
        adjoint = damping * adjoint + vbar * (alpha * (tilt + 2.0 * curve * u)) * (1.0 - u * u)
    a_ref[...] = adjoint
    zero = jnp.zeros((5, state.shape[1]), jnp.float32)
    slice_ids = par_ref[4:5, :]
    slice_rows = lax.broadcasted_iota(jnp.int32, (slices, state.shape[1]), 0).astype(jnp.float32)
    slice_table = jnp.where(slice_rows == slice_ids, 1.0, 0.0)
    g_ref[...] = lax.dot_general(
        jnp.concatenate(sums + [zero], axis=0),
        slice_table,
        NT,
        precision=PRECISE,
        preferred_element_type=jnp.float32,
    )


def local_part(xs, lt, params, trades, loss_given, width, slices):
    steps, paths, factors = xs.shape[0] - 1, xs.shape[1], xs.shape[2]
    blocks = factors // width
    tiles, _, tile = trades.shape
    rows, sets = steps * paths, loss_given.shape[0]
    return pl.pallas_call(
        local_kernel,
        out_shape=(
            jax.ShapeDtypeStruct((paths, factors), jnp.float32),
            jax.ShapeDtypeStruct((8, slices), jnp.float32),
        ),
        in_specs=[pl.BlockSpec(memory_space=pltpu.VMEM)] * 5,
        out_specs=(pl.BlockSpec(memory_space=pltpu.VMEM),) * 2,
        scratch_shapes=[
            pltpu.VMEM((steps, paths, factors), jnp.float32),
            pltpu.VMEM((blocks, rows, 3 * width), jnp.bfloat16),
            pltpu.VMEM((tiles, rows, tile), jnp.bfloat16),
            pltpu.VMEM((rows, sets), jnp.float32),
            pltpu.VMEM((blocks, rows, width), jnp.float32),
        ],
        compiler_params=pltpu.CompilerParams(vmem_limit_bytes=56 * 1024 * 1024),
    )(xs, lt, params, trades, loss_given[None, :])


def per_device(
    x_start,
    shocks,
    cholesky,
    reversion,
    sabr_alpha,
    sabr_rho,
    sabr_nu,
    factor_slice,
    notional,
    strike,
    trade_set,
    trade_factor,
    loss_given,
):
    width, path_cols = x_start.shape
    steps = shocks.shape[0]
    groups = lax.axis_size("factors")
    paths = path_cols // groups
    slice_count = sabr_alpha.shape[0]
    tile = min(TILE, notional.shape[0])
    floats = jnp.float32

    slice_table = (factor_slice[None, :] == jnp.arange(slice_count, dtype=jnp.int32)[:, None]).astype(
        floats
    )
    smile = jnp.dot(jnp.stack([sabr_alpha, sabr_rho, sabr_nu]), slice_table, precision=PRECISE)
    params = jnp.concatenate([smile, reversion[None, :], factor_slice.astype(floats)[None, :]], axis=0)
    params = jnp.pad(params, ((0, 3), (0, 0)))
    params = lax.all_gather(params, "factors", axis=1, tiled=True)

    local_factor = trade_factor - lax.axis_index("factors") * width
    trades = jnp.stack(
        [a.astype(floats).reshape(-1, tile) for a in (notional, strike, trade_set, local_factor)],
        axis=1,
    )
    trades = lax.all_gather(trades, "factors", axis=0, tiled=True)
    lt = lax.all_gather(cholesky.T.astype(jnp.bfloat16), "factors", axis=0, tiled=True)

    xs = jnp.concatenate([x_start[None], shocks], axis=0)
    xs = xs.reshape(steps + 1, width, groups, paths).transpose(2, 0, 3, 1)
    xs = lax.all_to_all(xs.reshape(groups, -1, 128), "factors", 0, 0, tiled=True)
    xs = xs.reshape(groups, steps + 1, paths, width).transpose(1, 2, 0, 3)
    xs = xs.reshape(steps + 1, paths, groups * width)

    adjoint, grads = local_part(xs, lt, params, trades, loss_given, width, slice_count)

    back = adjoint.reshape(paths, groups, width).transpose(1, 2, 0)
    back = lax.all_to_all(back.reshape(groups, -1, 128), "factors", 0, 0, tiled=True)
    back = back.reshape(groups, width, paths).transpose(1, 0, 2).reshape(width, path_cols)
    total = lax.psum(grads[:3], ("paths", "factors"))
    return back, total / (path_cols * lax.axis_size("paths"))


def solution(mesh):
    return jax.shard_map(
        per_device,
        mesh=mesh,
        in_specs=(
            P("factors", "paths"),
            P(None, "factors", "paths"),
            P(None, "factors"),
            P("factors"),
            P(),
            P(),
            P(),
            P("factors"),
            P("factors"),
            P("factors"),
            P("factors"),
            P("factors"),
            P(),
        ),
        out_specs=(P("factors", "paths"), P()),
        check_vma=False,
    )
```

```python
import functools
import math

import jax
import jax.numpy as jnp
from jax import lax
from jax.experimental import pallas as pl
from jax.experimental.pallas import tpu as pltpu
from jax.sharding import PartitionSpec as P

TIME_STEP = 0.25
ROOT_STEP = 0.5
DISCOUNT_RATE = 0.03
PRECISE = lax.Precision.HIGHEST
NN = (((1,), (0,)), ((), ()))
NT = (((1,), (1,)), ((), ()))
TILE = 512


def mm(a, b, dims):
    return lax.dot_general(a, b, dims, preferred_element_type=jnp.float32)


def split_mm(a, b, dims):
    rows = a.shape[0]
    high = a.astype(jnp.bfloat16)
    low = (a - high.astype(jnp.float32)).astype(jnp.bfloat16)
    both = mm(jnp.concatenate([high, low], axis=0), b, dims)
    return both[:rows] + both[rows:]


def one_hot(ids, count):
    rows = lax.broadcasted_iota(jnp.int32, (count, ids.shape[1]), 0).astype(jnp.float32)
    return jnp.where(rows == ids, 1.0, 0.0).astype(jnp.bfloat16)


def local_kernel(
    xs_ref,
    lt_ref,
    par_ref,
    trades_ref,
    loss_ref,
    a_ref,
    g_ref,
    states,
    parts,
    slopes,
    exposure,
    terms,
):
    steps = xs_ref.shape[0] - 1
    paths = xs_ref.shape[1]
    blocks, rows, part_width = parts.shape
    width = part_width // 3
    per_block = trades_ref.shape[1] - 1
    tiles = blocks * per_block
    sets = loss_ref.shape[1]
    slices = g_ref.shape[1]

    alpha, rho, nu = par_ref[0:1, :], par_ref[1:2, :], par_ref[2:3, :]
    damping = 1.0 - par_ref[3:4, :] * TIME_STEP
    curve2 = 2.0 - 3.0 * rho * rho
    curve = curve2 * nu * nu / 24.0
    tilt = 0.5 * rho * nu

    state = xs_ref[0]
    for k in range(steps):
        states[k] = state
        u = jnp.tanh(state)
        source = alpha * (1.0 + tilt * u + curve * u * u) * xs_ref[k + 1]
        state = damping * state + ROOT_STEP * split_mm(source, lt_ref[...], NN)
        high = state.astype(jnp.bfloat16)
        rest = state - high.astype(jnp.float32)
        mid = rest.astype(jnp.bfloat16)
        low = (rest - mid.astype(jnp.float32)).astype(jnp.bfloat16)
        for b in range(blocks):
            cols = slice(b * width, (b + 1) * width)
            parts[b, k * paths : (k + 1) * paths, :] = jnp.concatenate(
                [high[:, cols], mid[:, cols], low[:, cols]], axis=1
            )

    exposure[...] = jnp.zeros_like(exposure)

    def forward(i, carry):
        b, j = i // per_block, i % per_block
        notional = trades_ref[b, j, 0:1, :]
        strike = trades_ref[b, j, 1:2, :]
        table = one_hot(trades_ref[b, j, 3:4, :], width)
        money = mm(parts[b], jnp.concatenate([table, table, table], axis=0), NN) - strike
        squash = jnp.tanh(money)
        value = notional * squash
        slopes[i] = (notional - value * squash).astype(jnp.bfloat16)
        set_table = one_hot(trades_ref[b, j, 2:3, :], sets)
        exposure[...] += mm(value.astype(jnp.bfloat16), set_table, NT)
        return carry

    lax.fori_loop(0, tiles, forward, 0)

    weights = jnp.concatenate(
        [
            math.exp(-DISCOUNT_RATE * TIME_STEP * (k + 1))
            * loss_ref[...]
            * jax.nn.sigmoid(exposure[k * paths : (k + 1) * paths, :])
            for k in range(steps)
        ],
        axis=0,
    ).astype(jnp.bfloat16)
    terms[...] = jnp.zeros_like(terms)

    def backward(i, carry):
        b, j = i // per_block, i % per_block
        set_table = one_hot(trades_ref[b, j, 2:3, :], sets)
        pulled = slopes[i].astype(jnp.float32) * mm(weights, set_table, NN)
        table = one_hot(trades_ref[b, j, 3:4, :], width)
        terms[b] += mm(pulled.astype(jnp.bfloat16), table, NT)
        return carry

    lax.fori_loop(0, tiles, backward, 0)

    adjoint = jnp.zeros_like(state)
    sums = [jnp.zeros((1, state.shape[1]), jnp.float32) for _ in range(3)]
    for k in reversed(range(steps)):
        adjoint = adjoint + jnp.concatenate(
            [terms[b, k * paths : (k + 1) * paths, :] for b in range(blocks)], axis=1
        )
        u = jnp.tanh(states[k])
        vbar = split_mm(ROOT_STEP * adjoint, lt_ref[...], NT) * xs_ref[k + 1]
        for at, slope in enumerate(
            (
                1.0 + tilt * u + curve * u * u,
                alpha * (0.5 * nu * u - 0.25 * rho * nu * nu * u * u),
                alpha * (0.5 * rho * u + curve2 * nu * u * u / 12.0),
            )
        ):
            sums[at] = sums[at] + jnp.sum(vbar * slope, axis=0, keepdims=True)
        adjoint = damping * adjoint + vbar * (alpha * (tilt + 2.0 * curve * u)) * (1.0 - u * u)
    a_ref[...] = adjoint
    zero = jnp.zeros((5, state.shape[1]), jnp.float32)
    slice_ids = par_ref[4:5, :]
    slice_rows = lax.broadcasted_iota(jnp.int32, (slices, state.shape[1]), 0).astype(jnp.float32)
    slice_table = jnp.where(slice_rows == slice_ids, 1.0, 0.0)
    g_ref[...] = lax.dot_general(
        jnp.concatenate(sums + [zero], axis=0),
        slice_table,
        NT,
        precision=PRECISE,
        preferred_element_type=jnp.float32,
    )


def spread(block, axes):
    copies = jnp.broadcast_to(block[None], (lax.axis_size(axes),) + block.shape)
    return lax.all_to_all(copies, axes, 0, 0, tiled=True)


def local_part(xs, lt, params, trades, loss_given, width, slices):
    steps, paths, factors = xs.shape[0] - 1, xs.shape[1], xs.shape[2]
    blocks = factors // width
    tiles, tile = blocks * (trades.shape[1] - 1), trades.shape[3]
    rows, sets = steps * paths, loss_given.shape[0]
    return pl.pallas_call(
        local_kernel,
        out_shape=(
            jax.ShapeDtypeStruct((paths, factors), jnp.float32),
            jax.ShapeDtypeStruct((8, slices), jnp.float32),
        ),
        in_specs=[pl.BlockSpec(memory_space=pltpu.VMEM)] * 5,
        out_specs=(pl.BlockSpec(memory_space=pltpu.VMEM),) * 2,
        scratch_shapes=[
            pltpu.VMEM((steps, paths, factors), jnp.float32),
            pltpu.VMEM((blocks, rows, 3 * width), jnp.bfloat16),
            pltpu.VMEM((tiles, rows, tile), jnp.bfloat16),
            pltpu.VMEM((rows, sets), jnp.float32),
            pltpu.VMEM((blocks, rows, width), jnp.float32),
        ],
        compiler_params=pltpu.CompilerParams(vmem_limit_bytes=56 * 1024 * 1024),
    )(xs, lt, params, trades, loss_given[None, :])


def per_device(
    x_start,
    shocks,
    cholesky,
    reversion,
    sabr_alpha,
    sabr_rho,
    sabr_nu,
    factor_slice,
    notional,
    strike,
    trade_set,
    trade_factor,
    loss_given,
):
    width, path_cols = x_start.shape
    steps = shocks.shape[0]
    groups = lax.axis_size("factors")
    paths = path_cols // groups
    slice_count = sabr_alpha.shape[0]
    tile = min(TILE, notional.shape[0])
    floats = jnp.float32

    slice_table = (factor_slice[None, :] == jnp.arange(slice_count, dtype=jnp.int32)[:, None]).astype(
        floats
    )
    smile = jnp.dot(jnp.stack([sabr_alpha, sabr_rho, sabr_nu]), slice_table, precision=PRECISE)
    params = jnp.concatenate([smile, reversion[None, :], factor_slice.astype(floats)[None, :]], axis=0)
    params = params.reshape(-1)
    params = jnp.pad(params, (0, 4 * tile - params.shape[0])).reshape(1, 4, tile)

    local_factor = trade_factor - lax.axis_index("factors") * width
    trades = jnp.stack(
        [a.astype(floats).reshape(-1, tile) for a in (notional, strike, trade_set, local_factor)],
        axis=1,
    )
    trades = spread(jnp.concatenate([trades, params], axis=0), "factors")
    params = trades[:, -1].reshape(groups, -1)[:, : 5 * width].reshape(groups, 5, width)
    params = params.transpose(1, 0, 2).reshape(5, groups * width)
    lt = spread(cholesky.T.astype(jnp.bfloat16), "factors").reshape(-1, cholesky.shape[0])

    xs = jnp.concatenate([x_start[None], shocks], axis=0)
    xs = xs.reshape(steps + 1, width, groups, paths).transpose(2, 0, 3, 1)
    xs = lax.all_to_all(xs.reshape(groups, -1, 128), "factors", 0, 0, tiled=True)
    xs = xs.reshape(groups, steps + 1, paths, width).transpose(1, 2, 0, 3)
    xs = xs.reshape(steps + 1, paths, groups * width)

    adjoint, grads = local_part(xs, lt, params, trades, loss_given, width, slice_count)

    back = adjoint.reshape(paths, groups, width).transpose(1, 2, 0)
    back = lax.all_to_all(back.reshape(groups, -1, 128), "factors", 0, 0, tiled=True)
    back = back.reshape(groups, width, paths).transpose(1, 0, 2).reshape(width, path_cols)
    total = jnp.sum(spread(grads, ("paths", "factors")), axis=0)[:3]
    return back, total / (path_cols * lax.axis_size("paths"))


def solution(mesh):
    return jax.shard_map(
        per_device,
        mesh=mesh,
        in_specs=(
            P("factors", "paths"),
            P(None, "factors", "paths"),
            P(None, "factors"),
            P("factors"),
            P(),
            P(),
            P(),
            P("factors"),
            P("factors"),
            P("factors"),
            P("factors"),
            P("factors"),
            P(),
        ),
        out_specs=(P("factors", "paths"), P()),
        check_vma=False,
    )
```

```python
import functools
import math

import jax
import jax.numpy as jnp
from jax import lax
from jax.experimental import pallas as pl
from jax.experimental.pallas import tpu as pltpu
from jax.sharding import PartitionSpec as P

TIME_STEP = 0.25
ROOT_STEP = 0.5
DISCOUNT_RATE = 0.03
PRECISE = lax.Precision.HIGHEST
NN = (((1,), (0,)), ((), ()))
NT = (((1,), (1,)), ((), ()))
TILE = 512


def mm(a, b, dims):
    return lax.dot_general(a, b, dims, preferred_element_type=jnp.float32)


def split_mm(a, b, dims):
    rows = a.shape[0]
    high = a.astype(jnp.bfloat16)
    low = (a - high.astype(jnp.float32)).astype(jnp.bfloat16)
    both = mm(jnp.concatenate([high, low], axis=0), b, dims)
    return both[:rows] + both[rows:]


def one_hot(ids, count):
    rows = lax.broadcasted_iota(jnp.int32, (count, ids.shape[1]), 0).astype(jnp.float32)
    return jnp.where(rows == ids, 1.0, 0.0).astype(jnp.bfloat16)


def local_kernel(
    xs_ref,
    lt_ref,
    par_ref,
    trades_ref,
    loss_ref,
    a_ref,
    g_ref,
    states,
    parts,
    slopes,
    exposure,
    terms,
):
    steps = xs_ref.shape[0] - 1
    paths = xs_ref.shape[1]
    blocks, rows, part_width = parts.shape
    width = part_width // 3
    parts_of, per_part = trades_ref.shape[0], trades_ref.shape[2]
    per_block = parts_of * per_part
    tiles = blocks * per_block
    sets = loss_ref.shape[1]
    slices = g_ref.shape[1]

    alpha, rho, nu = par_ref[0:1, :], par_ref[1:2, :], par_ref[2:3, :]
    damping = 1.0 - par_ref[3:4, :] * TIME_STEP
    curve2 = 2.0 - 3.0 * rho * rho
    curve = curve2 * nu * nu / 24.0
    tilt = 0.5 * rho * nu

    state = xs_ref[0]
    for k in range(steps):
        states[k] = state
        u = jnp.tanh(state)
        source = alpha * (1.0 + tilt * u + curve * u * u) * xs_ref[k + 1]
        state = damping * state + ROOT_STEP * split_mm(source, lt_ref[...], NN)
        high = state.astype(jnp.bfloat16)
        rest = state - high.astype(jnp.float32)
        mid = rest.astype(jnp.bfloat16)
        low = (rest - mid.astype(jnp.float32)).astype(jnp.bfloat16)
        for b in range(blocks):
            cols = slice(b * width, (b + 1) * width)
            parts[b, k * paths : (k + 1) * paths, :] = jnp.concatenate(
                [high[:, cols], mid[:, cols], low[:, cols]], axis=1
            )

    exposure[...] = jnp.zeros_like(exposure)

    def forward(i, carry):
        b, j = i // per_block, i % per_block
        trade = trades_ref.at[j // per_part, b, j % per_part]
        notional = trade[0:1, :]
        strike = trade[1:2, :]
        table = one_hot(trade[3:4, :], width)
        money = mm(parts[b], jnp.concatenate([table, table, table], axis=0), NN) - strike
        squash = jnp.tanh(money)
        value = notional * squash
        slopes[i] = (notional - value * squash).astype(jnp.bfloat16)
        set_table = one_hot(trade[2:3, :], sets)
        exposure[...] += mm(value.astype(jnp.bfloat16), set_table, NT)
        return carry

    lax.fori_loop(0, tiles, forward, 0)

    weights = jnp.concatenate(
        [
            math.exp(-DISCOUNT_RATE * TIME_STEP * (k + 1))
            * loss_ref[...]
            * jax.nn.sigmoid(exposure[k * paths : (k + 1) * paths, :])
            for k in range(steps)
        ],
        axis=0,
    ).astype(jnp.bfloat16)
    terms[...] = jnp.zeros_like(terms)

    def backward(i, carry):
        b, j = i // per_block, i % per_block
        trade = trades_ref.at[j // per_part, b, j % per_part]
        set_table = one_hot(trade[2:3, :], sets)
        pulled = slopes[i].astype(jnp.float32) * mm(weights, set_table, NN)
        table = one_hot(trade[3:4, :], width)
        terms[b] += mm(pulled.astype(jnp.bfloat16), table, NT)
        return carry

    lax.fori_loop(0, tiles, backward, 0)

    adjoint = jnp.zeros_like(state)
    sums = [jnp.zeros((1, state.shape[1]), jnp.float32) for _ in range(3)]
    for k in reversed(range(steps)):
        adjoint = adjoint + jnp.concatenate(
            [terms[b, k * paths : (k + 1) * paths, :] for b in range(blocks)], axis=1
        )
        u = jnp.tanh(states[k])
        vbar = split_mm(ROOT_STEP * adjoint, lt_ref[...], NT) * xs_ref[k + 1]
        for at, slope in enumerate(
            (
                1.0 + tilt * u + curve * u * u,
                alpha * (0.5 * nu * u - 0.25 * rho * nu * nu * u * u),
                alpha * (0.5 * rho * u + curve2 * nu * u * u / 12.0),
            )
        ):
            sums[at] = sums[at] + jnp.sum(vbar * slope, axis=0, keepdims=True)
        adjoint = damping * adjoint + vbar * (alpha * (tilt + 2.0 * curve * u)) * (1.0 - u * u)
    a_ref[...] = adjoint
    zero = jnp.zeros((5, state.shape[1]), jnp.float32)
    slice_ids = par_ref[4:5, :]
    slice_rows = lax.broadcasted_iota(jnp.int32, (slices, state.shape[1]), 0).astype(jnp.float32)
    slice_table = jnp.where(slice_rows == slice_ids, 1.0, 0.0)
    g_ref[...] = lax.dot_general(
        jnp.concatenate(sums + [zero], axis=0),
        slice_table,
        NT,
        precision=PRECISE,
        preferred_element_type=jnp.float32,
    )


def spread(block, axes):
    copies = jnp.broadcast_to(block[None], (lax.axis_size(axes),) + block.shape)
    return lax.all_to_all(copies, axes, 0, 0, tiled=True)


def local_part(xs, lt, params, trades, loss_given, width, slices):
    steps, paths, factors = xs.shape[0] - 1, xs.shape[1], xs.shape[2]
    blocks = factors // width
    tiles, tile = blocks * trades.shape[0] * trades.shape[2], trades.shape[4]
    rows, sets = steps * paths, loss_given.shape[0]
    return pl.pallas_call(
        local_kernel,
        out_shape=(
            jax.ShapeDtypeStruct((paths, factors), jnp.float32),
            jax.ShapeDtypeStruct((8, slices), jnp.float32),
        ),
        in_specs=[pl.BlockSpec(memory_space=pltpu.VMEM)] * 5,
        out_specs=(pl.BlockSpec(memory_space=pltpu.VMEM),) * 2,
        scratch_shapes=[
            pltpu.VMEM((steps, paths, factors), jnp.float32),
            pltpu.VMEM((blocks, rows, 3 * width), jnp.bfloat16),
            pltpu.VMEM((tiles, rows, tile), jnp.bfloat16),
            pltpu.VMEM((rows, sets), jnp.float32),
            pltpu.VMEM((blocks, rows, width), jnp.float32),
        ],
        compiler_params=pltpu.CompilerParams(vmem_limit_bytes=56 * 1024 * 1024),
    )(xs, lt, params, trades, loss_given[None, :])


def barrier(groups, me, parts_of, part):
    sem = pltpu.get_barrier_semaphore()
    for o in range(1, groups):
        pl.semaphore_signal(
            sem, device_id={"factors": lax.rem(me + o, groups)}, device_id_type=pl.DeviceIdType.MESH
        )
    for o in range(1, parts_of):
        pl.semaphore_signal(
            sem, device_id={"paths": lax.rem(part + o, parts_of)}, device_id_type=pl.DeviceIdType.MESH
        )
    pl.semaphore_wait(sem, groups + parts_of - 2)


def send(source, target, send_sem, recv_sem, device):
    copy = pltpu.make_async_remote_copy(
        src_ref=source,
        dst_ref=target,
        send_sem=send_sem,
        recv_sem=recv_sem,
        device_id=device,
        device_id_type=pl.DeviceIdType.MESH,
    )
    copy.start()
    return copy


def fold(block):
    rows = block.shape[0] * block.shape[1] // 128
    return jnp.concatenate(
        [block[at : at + rows] for at in range(0, block.shape[0], rows)], axis=1
    )


def unfold(block, width):
    return jnp.concatenate([block[:, at : at + width] for at in range(0, 128, width)], axis=0)


def gather_kernel(
    groups,
    parts_of,
    x_ref,
    s_ref,
    par_ref,
    lt_ref,
    tr_ref,
    xs_out,
    par_out,
    lt_out,
    tr_out,
    xsend,
    xrecv,
    ltbuf,
    own_sem,
    lt_sem,
    tr_sem,
    x_sem,
    lt2_sem,
    tr2_sem,
):
    me, part = lax.axis_index("factors"), lax.axis_index("paths")
    width = x_ref.shape[0]
    paths = x_ref.shape[1] // groups
    count = s_ref.shape[0] + 1
    rows = paths * width // 128
    for a in range(count):
        turned = (x_ref[...] if a == 0 else s_ref[a - 1]).T
        for d in range(groups):
            xsend[d, a * rows : (a + 1) * rows, :] = fold(turned[d * paths : (d + 1) * paths])
    for d in range(groups):
        xsend[d, count * rows :, :] = par_ref[...]
    own = [
        pltpu.make_async_copy(lt_ref.at[part], ltbuf.at[part, me], own_sem.at[0]),
        pltpu.make_async_copy(tr_ref.at[part], tr_out.at[part, me], own_sem.at[1]),
    ]
    for copy in own:
        copy.start()
    barrier(groups, me, parts_of, part)
    lts, trs, xss = [], [], []
    for o in range(1, groups):
        device = {"factors": lax.rem(me + o, groups)}
        lts.append(send(lt_ref.at[part], ltbuf.at[part, me], lt_sem.at[0, o], lt_sem.at[1, o], device))
    for o in range(1, groups):
        device = {"factors": lax.rem(me + o, groups)}
        trs.append(send(tr_ref.at[part], tr_out.at[part, me], tr_sem.at[0, o], tr_sem.at[1, o], device))
    for o in range(1, groups):
        peer = lax.rem(me + o, groups)
        xss.append(
            send(xsend.at[peer], xrecv.at[me], x_sem.at[0, o], x_sem.at[1, o], {"factors": peer})
        )
    xrecv[me] = xsend[me]
    for copy in own:
        copy.wait()
    for copy in lts:
        copy.wait_recv()
    lt2, tr2 = [], []
    for o in range(1, parts_of):
        device = {"paths": lax.rem(part + o, parts_of)}
        lt2.append(send(ltbuf.at[part], ltbuf.at[part], lt2_sem.at[0, o], lt2_sem.at[1, o], device))
    for copy in trs:
        copy.wait_recv()
    for o in range(1, parts_of):
        device = {"paths": lax.rem(part + o, parts_of)}
        tr2.append(send(tr_out.at[part], tr_out.at[part], tr2_sem.at[0, o], tr2_sem.at[1, o], device))
    for copy in xss:
        copy.wait_recv()
    for a in range(count):
        xs_out[a] = jnp.concatenate(
            [unfold(xrecv[s, a * rows : (a + 1) * rows, :], width) for s in range(groups)], axis=1
        )
    par_out[...] = jnp.concatenate(
        [xrecv[s, count * rows :, :][:, :width] for s in range(groups)], axis=1
    )
    for copy in lt2:
        copy.wait_recv()
    per = lt_ref.shape[1]
    for s in range(groups):
        for q in range(parts_of):
            at = (s * parts_of + q) * per
            lt_out[at : at + per, :] = ltbuf[q, s]
    for copy in tr2:
        copy.wait_recv()
    for copy in lts + trs + xss + lt2 + tr2:
        copy.wait_send()


def gather_part(groups, parts_of, x_start, shocks, params, lt, trades):
    width, path_cols = x_start.shape
    paths, steps, factors = path_cols // groups, shocks.shape[0], groups * width
    rows = (steps + 1) * paths * width // 128 + 8
    vmem = pl.BlockSpec(memory_space=pltpu.VMEM)
    dma = pltpu.SemaphoreType.DMA
    return pl.pallas_call(
        functools.partial(gather_kernel, groups, parts_of),
        out_shape=(
            jax.ShapeDtypeStruct((steps + 1, paths, factors), jnp.float32),
            jax.ShapeDtypeStruct((8, factors), jnp.float32),
            jax.ShapeDtypeStruct((factors, factors), jnp.bfloat16),
            jax.ShapeDtypeStruct((parts_of, groups) + trades.shape[1:], jnp.float32),
        ),
        in_specs=[vmem] * 5,
        out_specs=(vmem,) * 4,
        scratch_shapes=[
            pltpu.VMEM((groups, rows, 128), jnp.float32),
            pltpu.VMEM((groups, rows, 128), jnp.float32),
            pltpu.VMEM((parts_of, groups) + lt.shape[1:], jnp.bfloat16),
            dma((2,)),
            dma((2, groups)),
            dma((2, groups)),
            dma((2, groups)),
            dma((2, parts_of)),
            dma((2, parts_of)),
        ],
        compiler_params=pltpu.CompilerParams(
            collective_id=0, has_side_effects=True, vmem_limit_bytes=32 * 1024 * 1024
        ),
    )(x_start, shocks, params, lt, trades)


def return_kernel(
    groups, parts_of, a_ref, g_ref, out_ref, gout_ref, asend, arecv, gbuf, a_sem, g_sem
):
    me, part = lax.axis_index("factors"), lax.axis_index("paths")
    paths = a_ref.shape[0]
    width = a_ref.shape[1] // groups
    rows = paths * width // 128
    turned = a_ref[...].T
    for d in range(groups):
        asend[d, :rows, :] = fold(turned[d * width : (d + 1) * width])
        asend[d, rows:, :] = g_ref[...]
    barrier(groups, me, parts_of, part)
    copies = []
    for o in range(1, groups):
        peer = lax.rem(me + o, groups)
        copies.append(
            send(asend.at[peer], arecv.at[me], a_sem.at[0, o], a_sem.at[1, o], {"factors": peer})
        )
    arecv[me] = asend[me]
    for copy in copies:
        copy.wait_recv()
    total = arecv[0, rows:, :]
    for s in range(1, groups):
        total = total + arecv[s, rows:, :]
    gbuf[part] = total
    sends = []
    for o in range(1, parts_of):
        device = {"paths": lax.rem(part + o, parts_of)}
        sends.append(send(gbuf.at[part], gbuf.at[part], g_sem.at[0, o], g_sem.at[1, o], device))
    out_ref[...] = jnp.concatenate(
        [unfold(arecv[s, :rows, :], paths) for s in range(groups)], axis=1
    )
    for copy in sends:
        copy.wait_recv()
    total = gbuf[0]
    for s in range(1, parts_of):
        total = total + gbuf[s]
    gout_ref[...] = total
    for copy in copies + sends:
        copy.wait_send()


def return_part(groups, parts_of, adjoint, grads):
    paths, factors = adjoint.shape
    width = factors // groups
    rows = paths * width // 128
    vmem = pl.BlockSpec(memory_space=pltpu.VMEM)
    dma = pltpu.SemaphoreType.DMA
    return pl.pallas_call(
        functools.partial(return_kernel, groups, parts_of),
        out_shape=(
            jax.ShapeDtypeStruct((width, groups * paths), jnp.float32),
            jax.ShapeDtypeStruct(grads.shape, jnp.float32),
        ),
        in_specs=[vmem] * 2,
        out_specs=(vmem,) * 2,
        scratch_shapes=[
            pltpu.VMEM((groups, rows + 8, 128), jnp.float32),
            pltpu.VMEM((groups, rows + 8, 128), jnp.float32),
            pltpu.VMEM((parts_of,) + grads.shape, jnp.float32),
            dma((2, groups)),
            dma((2, parts_of)),
        ],
        compiler_params=pltpu.CompilerParams(collective_id=1, has_side_effects=True),
    )(adjoint, grads)


def per_device(
    x_start,
    shocks,
    cholesky,
    reversion,
    sabr_alpha,
    sabr_rho,
    sabr_nu,
    factor_slice,
    notional,
    strike,
    trade_set,
    trade_factor,
    loss_given,
):
    width, path_cols = x_start.shape
    steps = shocks.shape[0]
    groups = lax.axis_size("factors")
    paths = path_cols // groups
    slice_count = sabr_alpha.shape[0]
    tile = min(TILE, notional.shape[0])
    floats = jnp.float32

    slice_table = (factor_slice[None, :] == jnp.arange(slice_count, dtype=jnp.int32)[:, None]).astype(
        floats
    )
    smile = jnp.dot(jnp.stack([sabr_alpha, sabr_rho, sabr_nu]), slice_table, precision=PRECISE)
    params = jnp.concatenate([smile, reversion[None, :], factor_slice.astype(floats)[None, :]], axis=0)
    local_factor = trade_factor - lax.axis_index("factors") * width
    trades = jnp.stack(
        [a.astype(floats).reshape(-1, tile) for a in (notional, strike, trade_set, local_factor)],
        axis=1,
    )
    lt = cholesky.T.astype(jnp.bfloat16)
    parts_of = lax.axis_size("paths")
    if (
        width == paths
        and width in (64, 128)
        and width % (16 * parts_of) == 0
        and trades.shape[0] % parts_of == 0
        and slice_count <= 128
    ):
        params = jnp.pad(params, ((0, 3), (0, 128 - width)))
        lt = lt.reshape(parts_of, width // parts_of, -1)
        trades = trades.reshape(parts_of, -1, 4, tile)
        xs, params, lt, trades = gather_part(
            groups, parts_of, x_start, shocks, params, lt, trades
        )
        adjoint, grads = local_part(xs, lt, params, trades, loss_given, width, 128)
        back, total = return_part(groups, parts_of, adjoint, grads)
        return back, total[:3, :slice_count] / (path_cols * parts_of)

    params = params.reshape(-1)
    params = jnp.pad(params, (0, 4 * tile - params.shape[0])).reshape(1, 4, tile)

    trades = spread(jnp.concatenate([trades, params], axis=0), "factors")
    params = trades[:, -1].reshape(groups, -1)[:, : 5 * width].reshape(groups, 5, width)
    params = params.transpose(1, 0, 2).reshape(5, groups * width)
    trades = trades[:, :-1][None]
    lt = spread(lt, "factors").reshape(-1, cholesky.shape[0])

    xs = jnp.concatenate([x_start[None], shocks], axis=0)
    xs = xs.reshape(steps + 1, width, groups, paths).transpose(2, 0, 3, 1)
    xs = lax.all_to_all(xs.reshape(groups, -1, 128), "factors", 0, 0, tiled=True)
    xs = xs.reshape(groups, steps + 1, paths, width).transpose(1, 2, 0, 3)
    xs = xs.reshape(steps + 1, paths, groups * width)

    adjoint, grads = local_part(xs, lt, params, trades, loss_given, width, slice_count)

    back = adjoint.reshape(paths, groups, width).transpose(1, 2, 0)
    back = lax.all_to_all(back.reshape(groups, -1, 128), "factors", 0, 0, tiled=True)
    back = back.reshape(groups, width, paths).transpose(1, 0, 2).reshape(width, path_cols)
    total = jnp.sum(spread(grads, ("paths", "factors")), axis=0)[:3]
    return back, total / (path_cols * lax.axis_size("paths"))


def solution(mesh):
    return jax.shard_map(
        per_device,
        mesh=mesh,
        in_specs=(
            P("factors", "paths"),
            P(None, "factors", "paths"),
            P(None, "factors"),
            P("factors"),
            P(),
            P(),
            P(),
            P("factors"),
            P("factors"),
            P("factors"),
            P("factors"),
            P("factors"),
            P(),
        ),
        out_specs=(P("factors", "paths"), P()),
        check_vma=False,
    )
```

```python
import functools
import math

import jax
import jax.numpy as jnp
from jax import lax
from jax.experimental import pallas as pl
from jax.experimental.pallas import tpu as pltpu
from jax.sharding import PartitionSpec as P

TIME_STEP = 0.25
ROOT_STEP = 0.5
DISCOUNT_RATE = 0.03
PRECISE = lax.Precision.HIGHEST
NN = (((1,), (0,)), ((), ()))
NT = (((1,), (1,)), ((), ()))
TILE = 1024
UNROLL = 4


def mm(a, b, dims):
    return lax.dot_general(a, b, dims, preferred_element_type=jnp.float32)


def split_mm(a, b, dims):
    rows = a.shape[0]
    high = a.astype(jnp.bfloat16)
    low = (a - high.astype(jnp.float32)).astype(jnp.bfloat16)
    both = mm(jnp.concatenate([high, low], axis=0), b, dims)
    return both[:rows] + both[rows:]


def one_hot(ids, count):
    shape = (16, ids.shape[1])
    near = jnp.broadcast_to(ids, shape).astype(jnp.int32) - lax.broadcasted_iota(jnp.int32, shape, 0)
    near = near.astype(jnp.int16)
    one, zero = jnp.ones(shape, jnp.bfloat16), jnp.zeros(shape, jnp.bfloat16)
    return jnp.concatenate(
        [jnp.where(near == jnp.int16(at), one, zero) for at in range(0, count, 16)], axis=0
    )


def local_kernel(
    xs_ref,
    lt_ref,
    par_ref,
    trades_ref,
    loss_ref,
    a_ref,
    g_ref,
    states,
    parts,
    slopes,
    exposure,
    terms,
):
    steps = xs_ref.shape[0] - 1
    paths = xs_ref.shape[1]
    blocks, rows, part_width = parts.shape
    width = part_width // 3
    parts_of, per_part = trades_ref.shape[0], trades_ref.shape[2]
    per_block = parts_of * per_part
    tiles = blocks * per_block
    sets = loss_ref.shape[1]
    slices = g_ref.shape[1]

    alpha, rho, nu = par_ref[0:1, :], par_ref[1:2, :], par_ref[2:3, :]
    damping = 1.0 - par_ref[3:4, :] * TIME_STEP
    curve2 = 2.0 - 3.0 * rho * rho
    curve = curve2 * nu * nu / 24.0
    tilt = 0.5 * rho * nu

    state = xs_ref[0]
    for k in range(steps):
        states[k] = state
        u = jnp.tanh(state)
        source = alpha * (1.0 + tilt * u + curve * u * u) * xs_ref[k + 1]
        state = damping * state + ROOT_STEP * split_mm(source, lt_ref[...], NN)
        high = state.astype(jnp.bfloat16)
        rest = state - high.astype(jnp.float32)
        mid = rest.astype(jnp.bfloat16)
        low = (rest - mid.astype(jnp.float32)).astype(jnp.bfloat16)
        for b in range(blocks):
            cols = slice(b * width, (b + 1) * width)
            parts[b, k * paths : (k + 1) * paths, :] = jnp.concatenate(
                [high[:, cols], mid[:, cols], low[:, cols]], axis=1
            )

    exposure[...] = jnp.zeros_like(exposure)

    def forward(i, carry):
        b, j = i // per_block, i % per_block
        trade = trades_ref.at[j // per_part, b, j % per_part]
        notional = trade[0:1, :]
        strike = trade[1:2, :]
        table = one_hot(trade[3:4, :], width)
        money = mm(parts[b], jnp.concatenate([table, table, table], axis=0), NN) - strike
        squash = jnp.tanh(money)
        value = notional * squash
        slopes[i] = (notional - value * squash).astype(jnp.bfloat16)
        set_table = one_hot(trade[2:3, :], sets)
        exposure[...] += mm(value.astype(jnp.bfloat16), set_table, NT)
        return carry

    lax.fori_loop(0, tiles, forward, 0, unroll=UNROLL)

    weights = jnp.concatenate(
        [
            math.exp(-DISCOUNT_RATE * TIME_STEP * (k + 1))
            * loss_ref[...]
            * jax.nn.sigmoid(exposure[k * paths : (k + 1) * paths, :])
            for k in range(steps)
        ],
        axis=0,
    ).astype(jnp.bfloat16)
    terms[...] = jnp.zeros_like(terms)

    def backward(i, carry):
        b, j = i // per_block, i % per_block
        trade = trades_ref.at[j // per_part, b, j % per_part]
        set_table = one_hot(trade[2:3, :], sets)
        pulled = slopes[i].astype(jnp.float32) * mm(weights, set_table, NN)
        table = one_hot(trade[3:4, :], width)
        terms[b] += mm(pulled.astype(jnp.bfloat16), table, NT)
        return carry

    lax.fori_loop(0, tiles, backward, 0, unroll=UNROLL)

    adjoint = jnp.zeros_like(state)
    sums = [jnp.zeros((1, state.shape[1]), jnp.float32) for _ in range(3)]
    for k in reversed(range(steps)):
        adjoint = adjoint + jnp.concatenate(
            [terms[b, k * paths : (k + 1) * paths, :] for b in range(blocks)], axis=1
        )
        u = jnp.tanh(states[k])
        vbar = split_mm(ROOT_STEP * adjoint, lt_ref[...], NT) * xs_ref[k + 1]
        for at, slope in enumerate(
            (
                1.0 + tilt * u + curve * u * u,
                alpha * (0.5 * nu * u - 0.25 * rho * nu * nu * u * u),
                alpha * (0.5 * rho * u + curve2 * nu * u * u / 12.0),
            )
        ):
            sums[at] = sums[at] + jnp.sum(vbar * slope, axis=0, keepdims=True)
        adjoint = damping * adjoint + vbar * (alpha * (tilt + 2.0 * curve * u)) * (1.0 - u * u)
    a_ref[...] = adjoint
    zero = jnp.zeros((5, state.shape[1]), jnp.float32)
    slice_ids = par_ref[4:5, :]
    slice_rows = lax.broadcasted_iota(jnp.int32, (slices, state.shape[1]), 0).astype(jnp.float32)
    slice_table = jnp.where(slice_rows == slice_ids, 1.0, 0.0)
    g_ref[...] = lax.dot_general(
        jnp.concatenate(sums + [zero], axis=0),
        slice_table,
        NT,
        precision=PRECISE,
        preferred_element_type=jnp.float32,
    )


def spread(block, axes):
    copies = jnp.broadcast_to(block[None], (lax.axis_size(axes),) + block.shape)
    return lax.all_to_all(copies, axes, 0, 0, tiled=True)


def local_part(xs, lt, params, trades, loss_given, width, slices):
    steps, paths, factors = xs.shape[0] - 1, xs.shape[1], xs.shape[2]
    blocks = factors // width
    tiles, tile = blocks * trades.shape[0] * trades.shape[2], trades.shape[4]
    rows, sets = steps * paths, loss_given.shape[0]
    return pl.pallas_call(
        local_kernel,
        out_shape=(
            jax.ShapeDtypeStruct((paths, factors), jnp.float32),
            jax.ShapeDtypeStruct((8, slices), jnp.float32),
        ),
        in_specs=[pl.BlockSpec(memory_space=pltpu.VMEM)] * 5,
        out_specs=(pl.BlockSpec(memory_space=pltpu.VMEM),) * 2,
        scratch_shapes=[
            pltpu.VMEM((steps, paths, factors), jnp.float32),
            pltpu.VMEM((blocks, rows, 3 * width), jnp.bfloat16),
            pltpu.VMEM((tiles, rows, tile), jnp.bfloat16),
            pltpu.VMEM((rows, sets), jnp.float32),
            pltpu.VMEM((blocks, rows, width), jnp.float32),
        ],
        compiler_params=pltpu.CompilerParams(vmem_limit_bytes=56 * 1024 * 1024),
    )(xs, lt, params, trades, loss_given[None, :])


def barrier(groups, me, parts_of, part):
    sem = pltpu.get_barrier_semaphore()
    for o in range(1, groups):
        pl.semaphore_signal(
            sem, device_id={"factors": lax.rem(me + o, groups)}, device_id_type=pl.DeviceIdType.MESH
        )
    for o in range(1, parts_of):
        pl.semaphore_signal(
            sem, device_id={"paths": lax.rem(part + o, parts_of)}, device_id_type=pl.DeviceIdType.MESH
        )
    pl.semaphore_wait(sem, groups + parts_of - 2)


def send(source, target, send_sem, recv_sem, device):
    copy = pltpu.make_async_remote_copy(
        src_ref=source,
        dst_ref=target,
        send_sem=send_sem,
        recv_sem=recv_sem,
        device_id=device,
        device_id_type=pl.DeviceIdType.MESH,
    )
    copy.start()
    return copy


def fold(block):
    rows = block.shape[0] * block.shape[1] // 128
    return jnp.concatenate(
        [block[at : at + rows] for at in range(0, block.shape[0], rows)], axis=1
    )


def unfold(block, width):
    return jnp.concatenate([block[:, at : at + width] for at in range(0, 128, width)], axis=0)


def gather_kernel(
    groups,
    parts_of,
    x_ref,
    s_ref,
    par_ref,
    lt_ref,
    tr_ref,
    xs_out,
    par_out,
    lt_out,
    tr_out,
    xsend,
    xrecv,
    ltbuf,
    own_sem,
    lt_sem,
    tr_sem,
    x_sem,
    lt2_sem,
    tr2_sem,
):
    me, part = lax.axis_index("factors"), lax.axis_index("paths")
    width = x_ref.shape[0]
    paths = x_ref.shape[1] // groups
    count = s_ref.shape[0] + 1
    rows = paths * width // 128
    for a in range(count):
        turned = (x_ref[...] if a == 0 else s_ref[a - 1]).T
        for d in range(groups):
            xsend[d, a * rows : (a + 1) * rows, :] = fold(turned[d * paths : (d + 1) * paths])
    for d in range(groups):
        xsend[d, count * rows :, :] = par_ref[...]
    own = [
        pltpu.make_async_copy(lt_ref.at[part], ltbuf.at[part, me], own_sem.at[0]),
        pltpu.make_async_copy(tr_ref.at[part], tr_out.at[part, me], own_sem.at[1]),
    ]
    for copy in own:
        copy.start()
    barrier(groups, me, parts_of, part)
    lts, trs, xss = [], [], []
    for o in range(1, groups):
        device = {"factors": lax.rem(me + o, groups)}
        lts.append(send(lt_ref.at[part], ltbuf.at[part, me], lt_sem.at[0, o], lt_sem.at[1, o], device))
    for o in range(1, groups):
        device = {"factors": lax.rem(me + o, groups)}
        trs.append(send(tr_ref.at[part], tr_out.at[part, me], tr_sem.at[0, o], tr_sem.at[1, o], device))
    for o in range(1, groups):
        peer = lax.rem(me + o, groups)
        xss.append(
            send(xsend.at[peer], xrecv.at[me], x_sem.at[0, o], x_sem.at[1, o], {"factors": peer})
        )
    xrecv[me] = xsend[me]
    for copy in own:
        copy.wait()
    for copy in lts:
        copy.wait_recv()
    lt2, tr2 = [], []
    for o in range(1, parts_of):
        device = {"paths": lax.rem(part + o, parts_of)}
        lt2.append(send(ltbuf.at[part], ltbuf.at[part], lt2_sem.at[0, o], lt2_sem.at[1, o], device))
    for copy in trs:
        copy.wait_recv()
    for o in range(1, parts_of):
        device = {"paths": lax.rem(part + o, parts_of)}
        tr2.append(send(tr_out.at[part], tr_out.at[part], tr2_sem.at[0, o], tr2_sem.at[1, o], device))
    for copy in xss:
        copy.wait_recv()
    for a in range(count):
        xs_out[a] = jnp.concatenate(
            [unfold(xrecv[s, a * rows : (a + 1) * rows, :], width) for s in range(groups)], axis=1
        )
    par_out[...] = jnp.concatenate(
        [xrecv[s, count * rows :, :][:, :width] for s in range(groups)], axis=1
    )
    for copy in lt2:
        copy.wait_recv()
    per = lt_ref.shape[1]
    for s in range(groups):
        for q in range(parts_of):
            at = (s * parts_of + q) * per
            lt_out[at : at + per, :] = ltbuf[q, s]
    for copy in tr2:
        copy.wait_recv()
    for copy in lts + trs + xss + lt2 + tr2:
        copy.wait_send()


def gather_part(groups, parts_of, x_start, shocks, params, lt, trades):
    width, path_cols = x_start.shape
    paths, steps, factors = path_cols // groups, shocks.shape[0], groups * width
    rows = (steps + 1) * paths * width // 128 + 8
    vmem = pl.BlockSpec(memory_space=pltpu.VMEM)
    dma = pltpu.SemaphoreType.DMA
    return pl.pallas_call(
        functools.partial(gather_kernel, groups, parts_of),
        out_shape=(
            jax.ShapeDtypeStruct((steps + 1, paths, factors), jnp.float32),
            jax.ShapeDtypeStruct((8, factors), jnp.float32),
            jax.ShapeDtypeStruct((factors, factors), jnp.bfloat16),
            jax.ShapeDtypeStruct((parts_of, groups) + trades.shape[1:], jnp.float32),
        ),
        in_specs=[vmem] * 5,
        out_specs=(vmem,) * 4,
        scratch_shapes=[
            pltpu.VMEM((groups, rows, 128), jnp.float32),
            pltpu.VMEM((groups, rows, 128), jnp.float32),
            pltpu.VMEM((parts_of, groups) + lt.shape[1:], jnp.bfloat16),
            dma((2,)),
            dma((2, groups)),
            dma((2, groups)),
            dma((2, groups)),
            dma((2, parts_of)),
            dma((2, parts_of)),
        ],
        compiler_params=pltpu.CompilerParams(
            collective_id=0, has_side_effects=True, vmem_limit_bytes=32 * 1024 * 1024
        ),
    )(x_start, shocks, params, lt, trades)


def return_kernel(
    groups, parts_of, a_ref, g_ref, out_ref, gout_ref, asend, arecv, gbuf, a_sem, g_sem
):
    me, part = lax.axis_index("factors"), lax.axis_index("paths")
    paths = a_ref.shape[0]
    width = a_ref.shape[1] // groups
    rows = paths * width // 128
    turned = a_ref[...].T
    for d in range(groups):
        asend[d, :rows, :] = fold(turned[d * width : (d + 1) * width])
        asend[d, rows:, :] = g_ref[...]
    barrier(groups, me, parts_of, part)
    copies = []
    for o in range(1, groups):
        peer = lax.rem(me + o, groups)
        copies.append(
            send(asend.at[peer], arecv.at[me], a_sem.at[0, o], a_sem.at[1, o], {"factors": peer})
        )
    arecv[me] = asend[me]
    for copy in copies:
        copy.wait_recv()
    total = arecv[0, rows:, :]
    for s in range(1, groups):
        total = total + arecv[s, rows:, :]
    gbuf[part] = total
    sends = []
    for o in range(1, parts_of):
        device = {"paths": lax.rem(part + o, parts_of)}
        sends.append(send(gbuf.at[part], gbuf.at[part], g_sem.at[0, o], g_sem.at[1, o], device))
    out_ref[...] = jnp.concatenate(
        [unfold(arecv[s, :rows, :], paths) for s in range(groups)], axis=1
    )
    for copy in sends:
        copy.wait_recv()
    total = gbuf[0]
    for s in range(1, parts_of):
        total = total + gbuf[s]
    gout_ref[...] = total
    for copy in copies + sends:
        copy.wait_send()


def return_part(groups, parts_of, adjoint, grads):
    paths, factors = adjoint.shape
    width = factors // groups
    rows = paths * width // 128
    vmem = pl.BlockSpec(memory_space=pltpu.VMEM)
    dma = pltpu.SemaphoreType.DMA
    return pl.pallas_call(
        functools.partial(return_kernel, groups, parts_of),
        out_shape=(
            jax.ShapeDtypeStruct((width, groups * paths), jnp.float32),
            jax.ShapeDtypeStruct(grads.shape, jnp.float32),
        ),
        in_specs=[vmem] * 2,
        out_specs=(vmem,) * 2,
        scratch_shapes=[
            pltpu.VMEM((groups, rows + 8, 128), jnp.float32),
            pltpu.VMEM((groups, rows + 8, 128), jnp.float32),
            pltpu.VMEM((parts_of,) + grads.shape, jnp.float32),
            dma((2, groups)),
            dma((2, parts_of)),
        ],
        compiler_params=pltpu.CompilerParams(collective_id=1, has_side_effects=True),
    )(adjoint, grads)


def per_device(
    x_start,
    shocks,
    cholesky,
    reversion,
    sabr_alpha,
    sabr_rho,
    sabr_nu,
    factor_slice,
    notional,
    strike,
    trade_set,
    trade_factor,
    loss_given,
):
    width, path_cols = x_start.shape
    steps = shocks.shape[0]
    groups = lax.axis_size("factors")
    paths = path_cols // groups
    slice_count = sabr_alpha.shape[0]
    tile = min(TILE, notional.shape[0])
    floats = jnp.float32

    slice_table = (factor_slice[None, :] == jnp.arange(slice_count, dtype=jnp.int32)[:, None]).astype(
        floats
    )
    smile = jnp.dot(jnp.stack([sabr_alpha, sabr_rho, sabr_nu]), slice_table, precision=PRECISE)
    params = jnp.concatenate([smile, reversion[None, :], factor_slice.astype(floats)[None, :]], axis=0)
    local_factor = trade_factor - lax.axis_index("factors") * width
    trades = jnp.stack(
        [a.astype(floats).reshape(-1, tile) for a in (notional, strike, trade_set, local_factor)],
        axis=1,
    )
    lt = cholesky.T.astype(jnp.bfloat16)
    parts_of = lax.axis_size("paths")
    if (
        width == paths
        and width in (64, 128)
        and width % (16 * parts_of) == 0
        and trades.shape[0] % parts_of == 0
        and slice_count <= 128
    ):
        params = jnp.pad(params, ((0, 3), (0, 128 - width)))
        lt = lt.reshape(parts_of, width // parts_of, -1)
        trades = trades.reshape(parts_of, -1, 4, tile)
        xs, params, lt, trades = gather_part(
            groups, parts_of, x_start, shocks, params, lt, trades
        )
        adjoint, grads = local_part(xs, lt, params, trades, loss_given, width, 128)
        back, total = return_part(groups, parts_of, adjoint, grads)
        return back, total[:3, :slice_count] / (path_cols * parts_of)

    params = params.reshape(-1)
    params = jnp.pad(params, (0, 4 * tile - params.shape[0])).reshape(1, 4, tile)

    trades = spread(jnp.concatenate([trades, params], axis=0), "factors")
    params = trades[:, -1].reshape(groups, -1)[:, : 5 * width].reshape(groups, 5, width)
    params = params.transpose(1, 0, 2).reshape(5, groups * width)
    trades = trades[:, :-1][None]
    lt = spread(lt, "factors").reshape(-1, cholesky.shape[0])

    xs = jnp.concatenate([x_start[None], shocks], axis=0)
    xs = xs.reshape(steps + 1, width, groups, paths).transpose(2, 0, 3, 1)
    xs = lax.all_to_all(xs.reshape(groups, -1, 128), "factors", 0, 0, tiled=True)
    xs = xs.reshape(groups, steps + 1, paths, width).transpose(1, 2, 0, 3)
    xs = xs.reshape(steps + 1, paths, groups * width)

    adjoint, grads = local_part(xs, lt, params, trades, loss_given, width, slice_count)

    back = adjoint.reshape(paths, groups, width).transpose(1, 2, 0)
    back = lax.all_to_all(back.reshape(groups, -1, 128), "factors", 0, 0, tiled=True)
    back = back.reshape(groups, width, paths).transpose(1, 0, 2).reshape(width, path_cols)
    total = jnp.sum(spread(grads, ("paths", "factors")), axis=0)[:3]
    return back, total / (path_cols * lax.axis_size("paths"))


def solution(mesh):
    return jax.shard_map(
        per_device,
        mesh=mesh,
        in_specs=(
            P("factors", "paths"),
            P(None, "factors", "paths"),
            P(None, "factors"),
            P("factors"),
            P(),
            P(),
            P(),
            P("factors"),
            P("factors"),
            P("factors"),
            P("factors"),
            P("factors"),
            P(),
        ),
        out_specs=(P("factors", "paths"), P()),
        check_vma=False,
    )
```

```python
import functools
import math

import jax
import jax.numpy as jnp
from jax import lax
from jax.experimental import pallas as pl
from jax.experimental.pallas import tpu as pltpu
from jax.sharding import PartitionSpec as P

TIME_STEP = 0.25
ROOT_STEP = 0.5
DISCOUNT_RATE = 0.03
PRECISE = lax.Precision.HIGHEST
NN = (((1,), (0,)), ((), ()))
NT = (((1,), (1,)), ((), ()))
TILE = 1024
UNROLL = 4


def mm(a, b, dims):
    return lax.dot_general(a, b, dims, preferred_element_type=jnp.float32)


def split_mm(a, b, dims):
    rows = a.shape[0]
    high = a.astype(jnp.bfloat16)
    low = (a - high.astype(jnp.float32)).astype(jnp.bfloat16)
    both = mm(jnp.concatenate([high, low], axis=0), b, dims)
    return both[:rows] + both[rows:]


def one_hot(ids, count):
    shape = (16, ids.shape[1])
    near = jnp.broadcast_to(ids, shape).astype(jnp.int32) - lax.broadcasted_iota(jnp.int32, shape, 0)
    near = near.astype(jnp.int16)
    one, zero = jnp.ones(shape, jnp.bfloat16), jnp.zeros(shape, jnp.bfloat16)
    return jnp.concatenate(
        [jnp.where(near == jnp.int16(at), one, zero) for at in range(0, count, 16)], axis=0
    )


def local_kernel(
    xs_ref,
    lt_ref,
    par_ref,
    trades_ref,
    loss_ref,
    a_ref,
    g_ref,
    states,
    parts,
    slopes,
    exposure,
    terms,
):
    steps = xs_ref.shape[0] - 1
    paths = xs_ref.shape[1]
    blocks, rows, part_width = parts.shape
    width = part_width // 3
    parts_of, per_part = trades_ref.shape[0], trades_ref.shape[2]
    per_block = parts_of * per_part
    tiles = blocks * per_block
    sets = loss_ref.shape[1]
    slices = g_ref.shape[1]

    alpha, rho, nu = par_ref[0:1, :], par_ref[1:2, :], par_ref[2:3, :]
    damping = 1.0 - par_ref[3:4, :] * TIME_STEP
    curve2 = 2.0 - 3.0 * rho * rho
    curve = curve2 * nu * nu / 24.0
    tilt = 0.5 * rho * nu

    state = xs_ref[0]
    for k in range(steps):
        states[k] = state
        u = jnp.tanh(state)
        source = alpha * (1.0 + tilt * u + curve * u * u) * xs_ref[k + 1]
        state = damping * state + ROOT_STEP * split_mm(source, lt_ref[...], NN)
        high = state.astype(jnp.bfloat16)
        rest = state - high.astype(jnp.float32)
        mid = rest.astype(jnp.bfloat16)
        low = (rest - mid.astype(jnp.float32)).astype(jnp.bfloat16)
        for b in range(blocks):
            cols = slice(b * width, (b + 1) * width)
            parts[b, k * paths : (k + 1) * paths, :] = jnp.concatenate(
                [high[:, cols], mid[:, cols], low[:, cols]], axis=1
            )

    exposure[...] = jnp.zeros_like(exposure)

    def forward(i, carry):
        b, j = i // per_block, i % per_block
        trade = trades_ref.at[j // per_part, b, j % per_part]
        notional = trade[0:1, :]
        strike = trade[1:2, :]
        table = one_hot(trade[3:4, :], width)
        money = mm(parts[b], jnp.concatenate([table, table, table], axis=0), NN) - strike
        squash = jnp.tanh(money)
        value = notional * squash
        slopes[i] = (notional - value * squash).astype(jnp.bfloat16)
        set_table = one_hot(trade[2:3, :], sets)
        exposure[...] += mm(value.astype(jnp.bfloat16), set_table, NT)
        return carry

    lax.fori_loop(0, tiles, forward, 0, unroll=UNROLL)

    weights = jnp.concatenate(
        [
            math.exp(-DISCOUNT_RATE * TIME_STEP * (k + 1))
            * loss_ref[...]
            * jax.nn.sigmoid(exposure[k * paths : (k + 1) * paths, :])
            for k in range(steps)
        ],
        axis=0,
    ).astype(jnp.bfloat16)
    terms[...] = jnp.zeros_like(terms)

    def backward(i, carry):
        b, j = i // per_block, i % per_block
        trade = trades_ref.at[j // per_part, b, j % per_part]
        set_table = one_hot(trade[2:3, :], sets)
        pulled = slopes[i].astype(jnp.float32) * mm(weights, set_table, NN)
        table = one_hot(trade[3:4, :], width)
        terms[b] += mm(pulled.astype(jnp.bfloat16), table, NT)
        return carry

    lax.fori_loop(0, tiles, backward, 0, unroll=UNROLL)

    adjoint = jnp.zeros_like(state)
    sums = [jnp.zeros((1, state.shape[1]), jnp.float32) for _ in range(3)]
    for k in reversed(range(steps)):
        adjoint = adjoint + jnp.concatenate(
            [terms[b, k * paths : (k + 1) * paths, :] for b in range(blocks)], axis=1
        )
        u = jnp.tanh(states[k])
        vbar = split_mm(ROOT_STEP * adjoint, lt_ref[...], NT) * xs_ref[k + 1]
        for at, slope in enumerate(
            (
                1.0 + tilt * u + curve * u * u,
                alpha * (0.5 * nu * u - 0.25 * rho * nu * nu * u * u),
                alpha * (0.5 * rho * u + curve2 * nu * u * u / 12.0),
            )
        ):
            sums[at] = sums[at] + jnp.sum(vbar * slope, axis=0, keepdims=True)
        adjoint = damping * adjoint + vbar * (alpha * (tilt + 2.0 * curve * u)) * (1.0 - u * u)
    a_ref[...] = adjoint
    zero = jnp.zeros((5, state.shape[1]), jnp.float32)
    slice_ids = par_ref[4:5, :]
    slice_rows = lax.broadcasted_iota(jnp.int32, (slices, state.shape[1]), 0).astype(jnp.float32)
    slice_table = jnp.where(slice_rows == slice_ids, 1.0, 0.0)
    g_ref[...] = lax.dot_general(
        jnp.concatenate(sums + [zero], axis=0),
        slice_table,
        NT,
        precision=PRECISE,
        preferred_element_type=jnp.float32,
    )


def spread(block, axes):
    copies = jnp.broadcast_to(block[None], (lax.axis_size(axes),) + block.shape)
    return lax.all_to_all(copies, axes, 0, 0, tiled=True)


def local_part(xs, lt, params, trades, loss_given, width, slices):
    steps, paths, factors = xs.shape[0] - 1, xs.shape[1], xs.shape[2]
    blocks = factors // width
    tiles, tile = blocks * trades.shape[0] * trades.shape[2], trades.shape[4]
    rows, sets = steps * paths, loss_given.shape[0]
    return pl.pallas_call(
        local_kernel,
        out_shape=(
            jax.ShapeDtypeStruct((paths, factors), jnp.float32),
            jax.ShapeDtypeStruct((8, slices), jnp.float32),
        ),
        in_specs=[pl.BlockSpec(memory_space=pltpu.VMEM)] * 5,
        out_specs=(pl.BlockSpec(memory_space=pltpu.VMEM),) * 2,
        scratch_shapes=[
            pltpu.VMEM((steps, paths, factors), jnp.float32),
            pltpu.VMEM((blocks, rows, 3 * width), jnp.bfloat16),
            pltpu.VMEM((tiles, rows, tile), jnp.bfloat16),
            pltpu.VMEM((rows, sets), jnp.float32),
            pltpu.VMEM((blocks, rows, width), jnp.float32),
        ],
        compiler_params=pltpu.CompilerParams(vmem_limit_bytes=56 * 1024 * 1024),
    )(xs, lt, params, trades, loss_given[None, :])


def barrier(groups, me, parts_of, part):
    sem = pltpu.get_barrier_semaphore()
    for o in range(1, groups):
        pl.semaphore_signal(
            sem, device_id={"factors": lax.rem(me + o, groups)}, device_id_type=pl.DeviceIdType.MESH
        )
    for o in range(1, parts_of):
        pl.semaphore_signal(
            sem, device_id={"paths": lax.rem(part + o, parts_of)}, device_id_type=pl.DeviceIdType.MESH
        )
    return functools.partial(pl.semaphore_wait, sem, groups + parts_of - 2)


def send(source, target, send_sem, recv_sem, device):
    copy = pltpu.make_async_remote_copy(
        src_ref=source,
        dst_ref=target,
        send_sem=send_sem,
        recv_sem=recv_sem,
        device_id=device,
        device_id_type=pl.DeviceIdType.MESH,
    )
    copy.start()
    return copy


def fold(block):
    rows = block.shape[0] * block.shape[1] // 128
    return jnp.concatenate(
        [block[at : at + rows] for at in range(0, block.shape[0], rows)], axis=1
    )


def unfold(block, width):
    return jnp.concatenate([block[:, at : at + width] for at in range(0, 128, width)], axis=0)


def gather_kernel(
    groups,
    parts_of,
    x_ref,
    s_ref,
    par_ref,
    lt_ref,
    tr_ref,
    xs_out,
    par_out,
    lt_out,
    tr_out,
    xsend,
    xrecv,
    ltbuf,
    own_sem,
    lt_sem,
    tr_sem,
    x_sem,
    lt2_sem,
    tr2_sem,
):
    me, part = lax.axis_index("factors"), lax.axis_index("paths")
    width = x_ref.shape[0]
    paths = x_ref.shape[1] // groups
    count = s_ref.shape[0] + 1
    rows = paths * width // 128
    for a in range(count):
        turned = (x_ref[...] if a == 0 else s_ref[a - 1]).T
        for d in range(groups):
            xsend[d, a * rows : (a + 1) * rows, :] = fold(turned[d * paths : (d + 1) * paths])
    for d in range(groups):
        xsend[d, count * rows :, :] = par_ref[...]
    own = [
        pltpu.make_async_copy(lt_ref.at[part], ltbuf.at[part, me], own_sem.at[0]),
        pltpu.make_async_copy(tr_ref.at[part], tr_out.at[part, me], own_sem.at[1]),
    ]
    for copy in own:
        copy.start()
    barrier(groups, me, parts_of, part)()
    lts, trs, xss = [], [], []
    for o in range(1, groups):
        device = {"factors": lax.rem(me + o, groups)}
        lts.append(send(lt_ref.at[part], ltbuf.at[part, me], lt_sem.at[0, o], lt_sem.at[1, o], device))
    for o in range(1, groups):
        device = {"factors": lax.rem(me + o, groups)}
        trs.append(send(tr_ref.at[part], tr_out.at[part, me], tr_sem.at[0, o], tr_sem.at[1, o], device))
    for o in range(1, groups):
        peer = lax.rem(me + o, groups)
        xss.append(
            send(xsend.at[peer], xrecv.at[me], x_sem.at[0, o], x_sem.at[1, o], {"factors": peer})
        )
    xrecv[me] = xsend[me]
    for copy in own:
        copy.wait()
    for copy in lts:
        copy.wait_recv()
    lt2, tr2 = [], []
    for o in range(1, parts_of):
        device = {"paths": lax.rem(part + o, parts_of)}
        lt2.append(send(ltbuf.at[part], ltbuf.at[part], lt2_sem.at[0, o], lt2_sem.at[1, o], device))
    for copy in trs:
        copy.wait_recv()
    for o in range(1, parts_of):
        device = {"paths": lax.rem(part + o, parts_of)}
        tr2.append(send(tr_out.at[part], tr_out.at[part], tr2_sem.at[0, o], tr2_sem.at[1, o], device))
    for copy in xss:
        copy.wait_recv()
    for a in range(count):
        xs_out[a] = jnp.concatenate(
            [unfold(xrecv[s, a * rows : (a + 1) * rows, :], width) for s in range(groups)], axis=1
        )
    par_out[...] = jnp.concatenate(
        [xrecv[s, count * rows :, :][:, :width] for s in range(groups)], axis=1
    )
    for copy in lt2:
        copy.wait_recv()
    per = lt_ref.shape[1]
    for s in range(groups):
        for q in range(parts_of):
            at = (s * parts_of + q) * per
            lt_out[at : at + per, :] = ltbuf[q, s]
    for copy in tr2:
        copy.wait_recv()
    for copy in lts + trs + xss + lt2 + tr2:
        copy.wait_send()


def gather_part(groups, parts_of, x_start, shocks, params, lt, trades):
    width, path_cols = x_start.shape
    paths, steps, factors = path_cols // groups, shocks.shape[0], groups * width
    rows = (steps + 1) * paths * width // 128 + 8
    vmem = pl.BlockSpec(memory_space=pltpu.VMEM)
    dma = pltpu.SemaphoreType.DMA
    return pl.pallas_call(
        functools.partial(gather_kernel, groups, parts_of),
        out_shape=(
            jax.ShapeDtypeStruct((steps + 1, paths, factors), jnp.float32),
            jax.ShapeDtypeStruct((8, factors), jnp.float32),
            jax.ShapeDtypeStruct((factors, factors), jnp.bfloat16),
            jax.ShapeDtypeStruct((parts_of, groups) + trades.shape[1:], jnp.float32),
        ),
        in_specs=[vmem] * 5,
        out_specs=(vmem,) * 4,
        scratch_shapes=[
            pltpu.VMEM((groups, rows, 128), jnp.float32),
            pltpu.VMEM((groups, rows, 128), jnp.float32),
            pltpu.VMEM((parts_of, groups) + lt.shape[1:], jnp.bfloat16),
            dma((2,)),
            dma((2, groups)),
            dma((2, groups)),
            dma((2, groups)),
            dma((2, parts_of)),
            dma((2, parts_of)),
        ],
        compiler_params=pltpu.CompilerParams(
            collective_id=0, has_side_effects=True, vmem_limit_bytes=32 * 1024 * 1024
        ),
    )(x_start, shocks, params, lt, trades)


def return_kernel(
    groups,
    parts_of,
    xs_ref,
    lt_ref,
    par_ref,
    trades_ref,
    loss_ref,
    out_ref,
    gout_ref,
    states,
    parts,
    slopes,
    exposure,
    terms,
    a_ref,
    g_ref,
    asend,
    arecv,
    gbuf,
    a_sem,
    g_sem,
):
    me, part = lax.axis_index("factors"), lax.axis_index("paths")
    all_in = barrier(groups, me, parts_of, part)
    local_kernel(
        xs_ref, lt_ref, par_ref, trades_ref, loss_ref, a_ref, g_ref,
        states, parts, slopes, exposure, terms,
    )
    paths = a_ref.shape[0]
    width = a_ref.shape[1] // groups
    rows = paths * width // 128
    turned = a_ref[...].T
    for d in range(groups):
        asend[d, :rows, :] = fold(turned[d * width : (d + 1) * width])
        asend[d, rows:, :] = g_ref[...]
    all_in()
    copies = []
    for o in range(1, groups):
        peer = lax.rem(me + o, groups)
        copies.append(
            send(asend.at[peer], arecv.at[me], a_sem.at[0, o], a_sem.at[1, o], {"factors": peer})
        )
    arecv[me] = asend[me]
    for copy in copies:
        copy.wait_recv()
    total = arecv[0, rows:, :]
    for s in range(1, groups):
        total = total + arecv[s, rows:, :]
    gbuf[part] = total
    sends = []
    for o in range(1, parts_of):
        device = {"paths": lax.rem(part + o, parts_of)}
        sends.append(send(gbuf.at[part], gbuf.at[part], g_sem.at[0, o], g_sem.at[1, o], device))
    out_ref[...] = jnp.concatenate(
        [unfold(arecv[s, :rows, :], paths) for s in range(groups)], axis=1
    )
    for copy in sends:
        copy.wait_recv()
    total = gbuf[0]
    for s in range(1, parts_of):
        total = total + gbuf[s]
    gout_ref[...] = total
    for copy in copies + sends:
        copy.wait_send()


def return_part(groups, parts_of, xs, lt, params, trades, loss_given):
    paths, factors = xs.shape[1], xs.shape[2]
    width = factors // groups
    rows = paths * width // 128
    batch, sets = (xs.shape[0] - 1) * paths, loss_given.shape[0]
    tiles, tile = groups * trades.shape[0] * trades.shape[2], trades.shape[4]
    vmem = pl.BlockSpec(memory_space=pltpu.VMEM)
    dma = pltpu.SemaphoreType.DMA
    return pl.pallas_call(
        functools.partial(return_kernel, groups, parts_of),
        out_shape=(
            jax.ShapeDtypeStruct((width, groups * paths), jnp.float32),
            jax.ShapeDtypeStruct((8, 128), jnp.float32),
        ),
        in_specs=[vmem] * 5,
        out_specs=(vmem,) * 2,
        scratch_shapes=[
            pltpu.VMEM((xs.shape[0] - 1, paths, factors), jnp.float32),
            pltpu.VMEM((groups, batch, 3 * width), jnp.bfloat16),
            pltpu.VMEM((tiles, batch, tile), jnp.bfloat16),
            pltpu.VMEM((batch, sets), jnp.float32),
            pltpu.VMEM((groups, batch, width), jnp.float32),
            pltpu.VMEM((paths, factors), jnp.float32),
            pltpu.VMEM((8, 128), jnp.float32),
            pltpu.VMEM((groups, rows + 8, 128), jnp.float32),
            pltpu.VMEM((groups, rows + 8, 128), jnp.float32),
            pltpu.VMEM((parts_of, 8, 128), jnp.float32),
            dma((2, groups)),
            dma((2, parts_of)),
        ],
        compiler_params=pltpu.CompilerParams(
            collective_id=1, has_side_effects=True, vmem_limit_bytes=56 * 1024 * 1024
        ),
    )(xs, lt, params, trades, loss_given[None, :])


def per_device(
    x_start,
    shocks,
    cholesky,
    reversion,
    sabr_alpha,
    sabr_rho,
    sabr_nu,
    factor_slice,
    notional,
    strike,
    trade_set,
    trade_factor,
    loss_given,
):
    width, path_cols = x_start.shape
    steps = shocks.shape[0]
    groups = lax.axis_size("factors")
    paths = path_cols // groups
    slice_count = sabr_alpha.shape[0]
    tile = min(TILE, notional.shape[0])
    floats = jnp.float32

    slice_table = (factor_slice[None, :] == jnp.arange(slice_count, dtype=jnp.int32)[:, None]).astype(
        floats
    )
    smile = jnp.dot(jnp.stack([sabr_alpha, sabr_rho, sabr_nu]), slice_table, precision=PRECISE)
    params = jnp.concatenate([smile, reversion[None, :], factor_slice.astype(floats)[None, :]], axis=0)
    local_factor = trade_factor - lax.axis_index("factors") * width
    trades = jnp.stack(
        [a.astype(floats).reshape(-1, tile) for a in (notional, strike, trade_set, local_factor)],
        axis=1,
    )
    lt = cholesky.T.astype(jnp.bfloat16)
    parts_of = lax.axis_size("paths")
    if (
        width == paths
        and width in (64, 128)
        and width % (16 * parts_of) == 0
        and trades.shape[0] % parts_of == 0
        and slice_count <= 128
    ):
        params = jnp.pad(params, ((0, 3), (0, 128 - width)))
        lt = lt.reshape(parts_of, width // parts_of, -1)
        trades = trades.reshape(parts_of, -1, 4, tile)
        xs, params, lt, trades = gather_part(
            groups, parts_of, x_start, shocks, params, lt, trades
        )
        back, total = return_part(groups, parts_of, xs, lt, params, trades, loss_given)
        return back, total[:3, :slice_count] / (path_cols * parts_of)

    params = params.reshape(-1)
    params = jnp.pad(params, (0, 4 * tile - params.shape[0])).reshape(1, 4, tile)

    trades = spread(jnp.concatenate([trades, params], axis=0), "factors")
    params = trades[:, -1].reshape(groups, -1)[:, : 5 * width].reshape(groups, 5, width)
    params = params.transpose(1, 0, 2).reshape(5, groups * width)
    trades = trades[:, :-1][None]
    lt = spread(lt, "factors").reshape(-1, cholesky.shape[0])

    xs = jnp.concatenate([x_start[None], shocks], axis=0)
    xs = xs.reshape(steps + 1, width, groups, paths).transpose(2, 0, 3, 1)
    xs = lax.all_to_all(xs.reshape(groups, -1, 128), "factors", 0, 0, tiled=True)
    xs = xs.reshape(groups, steps + 1, paths, width).transpose(1, 2, 0, 3)
    xs = xs.reshape(steps + 1, paths, groups * width)

    adjoint, grads = local_part(xs, lt, params, trades, loss_given, width, slice_count)

    back = adjoint.reshape(paths, groups, width).transpose(1, 2, 0)
    back = lax.all_to_all(back.reshape(groups, -1, 128), "factors", 0, 0, tiled=True)
    back = back.reshape(groups, width, paths).transpose(1, 0, 2).reshape(width, path_cols)
    total = jnp.sum(spread(grads, ("paths", "factors")), axis=0)[:3]
    return back, total / (path_cols * lax.axis_size("paths"))


def solution(mesh):
    return jax.shard_map(
        per_device,
        mesh=mesh,
        in_specs=(
            P("factors", "paths"),
            P(None, "factors", "paths"),
            P(None, "factors"),
            P("factors"),
            P(),
            P(),
            P(),
            P("factors"),
            P("factors"),
            P("factors"),
            P("factors"),
            P("factors"),
            P(),
        ),
        out_specs=(P("factors", "paths"), P()),
        check_vma=False,
    )
```
